32 devices in a mesh: blk: 16 (over z, y, x), feat: 2 (over core).
Axes of the slice: x: 2, y: 2, z: 4, core: 2. Of those that a mesh axis runs over, the one named last changes fastest.
Arguments:
- points: bfloat16 [16384, 64], P('blk', 'feat'), may hold values from -1.5 to 1.5
- vectors: bfloat16 [16384, 64], P('blk', 'feat'), may hold values from -5.5 to 5.5
- lengthscale: float32 [64], replicated, may hold values from 0.5 to 2
- outscale: float32 [1], replicated, may hold values from 0.1 to 0.4
- noise: float32 [1], replicated, may hold values from 0.05 to 0.5
Outputs:
- product: float32 [16384, 64], P('blk', 'feat')
The draws below stay inside these ranges and needn't reach their ends.
All inputs are finite; a program needn't handle non-finite values.
Results may differ from the reference program's by a relative error of at most 0.0026.
Values may be sent and summed in bfloat16 or wider, within the bound.
A program may use at most 64 MiB of HBM per device.

```python
import math
import jax
import jax.numpy as jnp
from jax import lax

FEATS = 64
VECS = 64
PTS_DEV = 1024
POINTS = 16384


def draw_points(key, part):
    latent_width = FEATS // 4
    key_latent, key_map, key_noise, key_level = jax.random.split(jax.random.fold_in(key, 7), 4)
    spread = (0.5 / (FEATS * 1.35)) ** 0.5
    mapping = jax.random.normal(key_map, (latent_width, FEATS), jnp.float32) * spread
    jitter_level = jnp.exp(jax.random.uniform(key_level, (POINTS, 1), jnp.float32, math.log(0.04), math.log(0.3)))
    latent = jax.random.normal(key_latent, (POINTS, latent_width), jnp.float32)
    jitter = jax.random.normal(key_noise, (POINTS, FEATS), jnp.float32) * jitter_level
    values = jnp.dot(latent, mapping) + jitter
    return jnp.clip(values, -1.5, 1.5).astype(jnp.bfloat16)


def draw_vectors(key, part):
    key_noise, key_sign, key_size = jax.random.split(jax.random.fold_in(key, 11), 3)
    signs = jnp.where(jax.random.bernoulli(key_sign, 0.5, (VECS,)), 1.0, -1.0).astype(jnp.float32)
    offsets = signs * jax.random.uniform(key_size, (VECS,), jnp.float32, 0.75, 1.5)
    spread_part = jnp.clip(jax.random.normal(key_noise, (POINTS, VECS), jnp.float32), -4.0, 4.0)
    return (spread_part + offsets[None, :]).astype(jnp.bfloat16)


def setup_inputs(seed: int = 0) -> dict:
    key_of = jax.random.split(jax.random.key(seed), 6)
    return {
        "points": draw_points(jax.random.fold_in(key_of[5], 71), 0),
        "vectors": draw_vectors(jax.random.fold_in(key_of[5], 71), 0),
        "lengthscale": jnp.clip(jnp.exp(jax.random.uniform(key_of[2], (FEATS,), jnp.float32, math.log(0.5), math.log(2.0))), 0.5, 2.0),
        "outscale": jnp.clip(jnp.exp(jax.random.uniform(key_of[3], (1,), jnp.float32, math.log(0.1), math.log(0.4))), 0.1, 0.4),
        "noise": jnp.clip(jnp.exp(jax.random.uniform(key_of[4], (1,), jnp.float32, math.log(0.05), math.log(0.5))), 0.05, 0.5),
    }


def reference(points, vectors, lengthscale, outscale, noise):
    scaled = (points.astype(jnp.float32) / lengthscale).astype(jnp.bfloat16).astype(jnp.float32)
    norms = jnp.sum(scaled * scaled, axis=1)
    vector_wide = vectors.astype(jnp.float32)
    row_blocks = scaled.reshape(POINTS // PTS_DEV, PTS_DEV, FEATS)
    norm_blocks = norms.reshape(POINTS // PTS_DEV, PTS_DEV)

    def one_block(paired):
        block_rows, block_norms = paired
        inner = jnp.dot(block_rows, scaled.T, precision=lax.Precision.HIGHEST)
        distance = jnp.maximum(block_norms[:, None] + norms[None, :] - 2.0 * inner, 0.0)
        kernel_block = (outscale[0] * jnp.exp(-0.5 * distance)).astype(jnp.bfloat16).astype(jnp.float32)
        return jnp.dot(kernel_block, vector_wide, precision=lax.Precision.HIGHEST)

    result = lax.map(one_block, (row_blocks, norm_blocks)).reshape(POINTS, VECS)
    return result + noise[0] * vector_wide
```

```python
import functools

import jax
import jax.numpy as jnp
from jax import lax
from jax.experimental import pallas as pl
from jax.experimental.pallas import tpu as pltpu
from jax.sharding import PartitionSpec as P

LOG2E = 1.4426950408889634
F32 = jnp.float32
BF16 = jnp.bfloat16
EXTRA = 16
PLANE = 4


def pieces(value):
    first = value.astype(BF16).astype(F32)
    rest = value - first
    second = rest.astype(BF16).astype(F32)
    return first, second, rest - second


def extra_rows(rows):
    shape = (EXTRA, rows[0].shape[1])
    place = lax.broadcasted_iota(jnp.int32, shape, 0)
    out = jnp.zeros(shape, F32)
    for index, row in enumerate(rows):
        out = jnp.where(place == index, row, out)
    return out.astype(BF16)


def kernel(
    line, points, vectors, lengths_in, outscale_in, noise_in, result,
    lengths, outscale, noise, small_sem,
    columns, row_points, right, left, total, part_out, inbox, mine, swap_out, swap_in,
    twin_alive, plane_alive, line_alive,
    local_sem, pair_send, pair_recv, plane_send, plane_recv, twin_send, twin_recv,
    row_send, row_recv, part_send, part_recv, swap_send, swap_recv,
):
    me = lax.axis_index("blk")
    core = lax.axis_index("feat")
    other = 1 - core
    half, rows = points.shape
    feats = 2 * half
    share = rows // 2
    spot = me % PLANE
    level = me // PLANE

    def remote(src, dst, send, arrive, blk, feat):
        return pltpu.make_async_remote_copy(
            src_ref=src, dst_ref=dst, send_sem=send, recv_sem=arrive,
            device_id={"blk": blk, "feat": feat}, device_id_type=pl.DeviceIdType.MESH,
        )

    def signal(sem, blk, feat):
        pl.semaphore_signal(
            sem, inc=1, device_id={"blk": blk, "feat": feat},
            device_id_type=pl.DeviceIdType.MESH,
        )

    def plane_peer(index):
        return me ^ index

    def line_peer(step):
        return me ^ (step * PLANE)

    def loop(first, last, body):
        def one(index, carry):
            body(index)
            return carry
        lax.fori_loop(first, last, one, 0)

    small = [
        pltpu.make_async_copy(lengths_in, lengths, small_sem.at[0]),
        pltpu.make_async_copy(outscale_in, outscale, small_sem.at[1]),
        pltpu.make_async_copy(noise_in, noise, small_sem.at[2]),
    ]
    my_rows = pl.ds(pl.multiple_of(core * half, half), half)
    other_rows = pl.ds(pl.multiple_of(other * half, half), half)
    my_cols = pl.ds(pl.multiple_of(core * share, share), share)
    other_cols = pl.ds(pl.multiple_of(other * share, share), share)
    inputs = (points, vectors)
    locals_ = [
        pltpu.make_async_copy(array, columns.at[0, kind, my_rows, :], local_sem.at[kind])
        for kind, array in enumerate(inputs)
    ]
    locals_.append(pltpu.make_async_copy(vectors, mine, local_sem.at[2]))
    for copy in small + locals_:
        copy.start()

    barrier = pltpu.get_barrier_semaphore()

    @pl.when(core == 0)
    def _():
        signal(barrier, me, other)

    for index in range(1, PLANE):
        @pl.when(plane_peer(index) > me)
        def _():
            signal(barrier, plane_peer(index), core)

    def greet_line(step):
        @pl.when(line_peer(step) > me)
        def _():
            for feat in range(2):
                signal(barrier, line_peer(step), feat)

    loop(1, line, greet_line)
    before = core + spot + 2 * level

    @pl.when(before > 0)
    def _():
        pl.semaphore_wait(barrier, before)

    @pl.when(core == 1)
    def _():
        signal(twin_alive, me, other)

    for index in range(1, PLANE):
        @pl.when(plane_peer(index) < me)
        def _():
            signal(plane_alive.at[index], plane_peer(index), core)

    def answer_line(step):
        @pl.when(line_peer(step) < me)
        def _():
            for feat in range(2):
                signal(line_alive.at[step, core], line_peer(step), feat)

    loop(1, line, answer_line)

    pair = [
        remote(array, columns.at[0, kind, my_rows, :], pair_send.at[kind], pair_recv.at[kind],
               me, other)
        for kind, array in enumerate(inputs)
    ]

    def plane_copy(index, kind):
        return remote(inputs[kind], columns.at[index, kind, my_rows, :],
                      plane_send.at[index, kind], plane_recv.at[index, kind],
                      plane_peer(index), core)

    def twin(index, kind):
        place = columns.at[index, kind, my_rows, :]
        return remote(place, place, twin_send.at[index, kind], twin_recv.at[index, kind],
                      me, other)

    def row_copy(step, feat):
        return remote(points.at[:, feat * share:(feat + 1) * share],
                      row_points.at[step, my_rows, :],
                      row_send.at[step, feat], row_recv.at[step, core],
                      line_peer(step), feat)

    def row_arrival(step, feat):
        spots = pl.ds(feat * half, half)
        return remote(points.at[:, 0:share], row_points.at[step, spots, :],
                      row_send.at[step, feat], row_recv.at[step, feat],
                      line_peer(step), feat)

    def send_plane(index):
        for kind in range(2):
            plane_copy(index, kind).start()

    for index in range(1, PLANE):
        @pl.when(plane_peer(index) < me)
        def _():
            send_plane(index)

    def send_low(step):
        @pl.when(line_peer(step) < me)
        def _():
            for feat in range(2):
                row_copy(step, feat).start()

    loop(1, line, send_low)

    @pl.when(core == 0)
    def _():
        pl.semaphore_wait(twin_alive, 1)

    for copy in pair:
        copy.start()

    for index in range(1, PLANE):
        @pl.when(plane_peer(index) > me)
        def _():
            pl.semaphore_wait(plane_alive.at[index], 1)
            send_plane(index)

    def send_high(step):
        @pl.when(line_peer(step) > me)
        def _():
            for feat in range(2):
                pl.semaphore_wait(line_alive.at[step, feat], 1)
                row_copy(step, feat).start()

    for copy in small:
        copy.wait()
    scale = outscale[0]
    top = jnp.log(jnp.full((1, 1), scale, F32)) * LOG2E
    column = jnp.transpose(jnp.broadcast_to(lengths[...], (feats, feats)))[:, 0:1]

    for copy in locals_:
        copy.wait()
    for copy in pair:
        copy.wait_recv()

    def prepare_columns(index):
        for part in range(2):
            cols = slice(part * share, (part + 1) * share)
            guest = (columns[index, 0, :, cols].astype(F32) / column).astype(BF16)
            wide = guest.astype(F32)
            norm = -0.5 * LOG2E * jnp.sum(wide * wide, axis=0, keepdims=True)
            one = jnp.ones_like(norm)
            stacked = jnp.concatenate(
                [guest, guest, guest, extra_rows(pieces(norm) + (one, one, one))], axis=0)
            right[index, cols, :] = stacked.T

    def prepare_rows(step, value):
        scaled = (value.astype(F32) / column).astype(BF16).astype(F32)
        height = -0.5 * LOG2E * jnp.sum(scaled * scaled, axis=0, keepdims=True) + top
        one = jnp.ones_like(height)
        for index, piece in enumerate(pieces(scaled * LOG2E)):
            left[step, index * feats:(index + 1) * feats, :] = piece.astype(BF16)
        left[step, 3 * feats:, :] = extra_rows((one, one, one) + pieces(height))

    def unit(step, index):
        power = jnp.dot(right[index], left[step], preferred_element_type=F32)
        value = jnp.exp2(jnp.minimum(power, top)).astype(BF16)
        return jnp.dot(columns[index, 1], value, preferred_element_type=F32)

    def give_back(step, feat):
        return remote(part_out.at[step, feat], inbox.at[step, core],
                      part_send.at[step, feat], part_recv.at[step, core],
                      line_peer(step), feat)

    def back_arrival(step, feat):
        return remote(part_out.at[step, feat], inbox.at[step, feat],
                      part_send.at[step, feat], part_recv.at[step, feat],
                      line_peer(step), feat)

    def forward(index):
        for kind in range(2):
            plane_copy(index, kind).wait_recv()
            twin(index, kind).start()

    prepare_columns(0)

    def first(step):
        @pl.when(step == 0)
        def _():
            prepare_rows(step, columns[0, 0, :, my_cols])

        @pl.when(step == 1)
        def _():
            loop(1, line, send_high)
            forward(1)
            forward(2)

        @pl.when(step == 2)
        def _():
            forward(3)

        @pl.when(step > 0)
        def _():
            for feat in range(2):
                row_arrival(step, feat).wait_recv()
            prepare_rows(step, row_points[step])

        total[step] = unit(step, 0)

    loop(0, line, first)

    def rest(place):
        step = jnp.where(
            place < line - 1, level ^ (place + jnp.where(place >= level, 1, 0)), 0)

        def one_column(index):
            @pl.when(place == 0)
            def _():
                for kind in range(2):
                    twin(index, kind).wait_recv()
                prepare_columns(index)

            total[step] += unit(step, index)

        loop(1, PLANE, one_column)

        @pl.when(place < line - 1)
        def _():
            for feat in range(2):
                part_out[step, feat] = (
                    total[step, feat * half:(feat + 1) * half, :].astype(BF16))
            for feat in range(2):
                give_back(step, feat).start()

    loop(0, line, rest)

    swap_out[...] = total[0, other_rows, :]
    swap = remote(swap_out, swap_in, swap_send, swap_recv, me, other)
    swap.start()
    factor = noise[0]
    result[:, my_cols] = total[0, my_rows, :] + factor * mine[:, my_cols].astype(F32)
    result[:, other_cols] = factor * mine[:, other_cols].astype(F32)

    def collect(step):
        for feat in range(2):
            back_arrival(step, feat).wait_recv()
            result[:, feat * share:(feat + 1) * share] += inbox[step, feat].astype(F32)

    loop(1, line, collect)
    swap.wait_recv()
    result[:, other_cols] += swap_in[...]

    swap.wait_send()
    for copy in pair:
        copy.wait_send()
    for index in range(1, PLANE):
        for kind in range(2):
            plane_copy(index, kind).wait_send()
            twin(index, kind).wait_send()

    def drain(step):
        for feat in range(2):
            give_back(step, feat).wait_send()
            row_copy(step, feat).wait_send()

    loop(1, line, drain)


def per_device(blk, points, vectors, lengthscale, outscale, noise):
    assert blk % (4 * PLANE) == 0 and blk & (blk - 1) == 0
    line = blk // PLANE
    rows, half = points.shape
    feats = 2 * half
    share = rows // 2
    stay = pl.BlockSpec(memory_space=pltpu.HBM)
    vmem = pl.BlockSpec(memory_space=pltpu.VMEM)
    dma = pltpu.SemaphoreType.DMA
    regular = pltpu.SemaphoreType.REGULAR
    wide = 3 * feats + EXTRA
    out = pl.pallas_call(
        functools.partial(kernel, line),
        out_shape=pltpu.VMEM((half, rows), F32),
        in_specs=[stay] * 5,
        out_specs=vmem,
        scratch_shapes=[
            pltpu.VMEM((1, feats), F32),
            pltpu.SMEM((1,), F32),
            pltpu.SMEM((1,), F32),
            dma((3,)),
            pltpu.VMEM((PLANE, 2, feats, rows), BF16),
            pltpu.VMEM((line, feats, share), BF16),
            pltpu.VMEM((PLANE, rows, wide), BF16),
            pltpu.VMEM((line, wide, share), BF16),
            pltpu.VMEM((line, feats, share), F32),
            pltpu.VMEM((line, 2, half, share), BF16),
            pltpu.VMEM((line, 2, half, share), BF16),
            pltpu.VMEM((half, rows), BF16),
            pltpu.VMEM((half, share), F32),
            pltpu.VMEM((half, share), F32),
            regular,
            regular((PLANE,)),
            regular((line, 2)),
            dma((3,)),
            dma((2,)),
            dma((2,)),
            dma((PLANE, 2)),
            dma((PLANE, 2)),
            dma((PLANE, 2)),
            dma((PLANE, 2)),
            dma((line, 2)),
            dma((line, 2)),
            dma((line, 2)),
            dma((line, 2)),
            dma,
            dma,
        ],
        compiler_params=pltpu.CompilerParams(collective_id=0, has_side_effects=True),
        name="tile_solve",
    )(points.T, vectors.T, lengthscale.reshape(1, feats), outscale, noise)
    return out.T


def solution(mesh):
    placed = (P("blk", "feat"), P("blk", "feat"), P(), P(), P())
    return jax.shard_map(
        functools.partial(per_device, mesh.shape["blk"]),
        mesh=mesh, in_specs=placed, out_specs=P("blk", "feat"), check_vma=False,
    )
```

```python
import functools

import jax
import jax.numpy as jnp
from jax import lax
from jax.experimental import pallas as pl
from jax.experimental.pallas import tpu as pltpu
from jax.sharding import PartitionSpec as P

LOG2E = 1.4426950408889634
F32 = jnp.float32
BF16 = jnp.bfloat16
EXTRA = 16
PLANE = 4


def pieces(value):
    first = value.astype(BF16).astype(F32)
    rest = value - first
    second = rest.astype(BF16).astype(F32)
    return first, second, rest - second


def extra_rows(rows):
    shape = (EXTRA, rows[0].shape[1])
    place = lax.broadcasted_iota(jnp.int32, shape, 0)
    out = jnp.zeros(shape, F32)
    for index, row in enumerate(rows):
        out = jnp.where(place == index, row, out)
    return out.astype(BF16)


def kernel(
    line, points, vectors, lengths_in, outscale_in, noise_in, result,
    lengths, outscale, noise, small_sem,
    columns, row_points, right, left, total, part_out, inbox, mine, swap_out, swap_in,
    twin_alive, plane_alive, line_alive,
    local_sem, pair_send, pair_recv, plane_send, plane_recv, twin_send, twin_recv,
    row_send, row_recv, part_send, part_recv, swap_send, swap_recv,
):
    me = lax.axis_index("blk")
    core = lax.axis_index("feat")
    other = 1 - core
    half, rows = points.shape
    feats = 2 * half
    share = rows // 2
    spot = me % PLANE
    level = me // PLANE

    def remote(src, dst, send, arrive, blk, feat):
        return pltpu.make_async_remote_copy(
            src_ref=src, dst_ref=dst, send_sem=send, recv_sem=arrive,
            device_id={"blk": blk, "feat": feat}, device_id_type=pl.DeviceIdType.MESH,
        )

    def signal(sem, blk, feat):
        pl.semaphore_signal(
            sem, inc=1, device_id={"blk": blk, "feat": feat},
            device_id_type=pl.DeviceIdType.MESH,
        )

    def plane_peer(index):
        return me ^ index

    def line_peer(step):
        return me ^ (step * PLANE)

    def loop(first, last, body):
        def one(index, carry):
            body(index)
            return carry
        lax.fori_loop(first, last, one, 0)

    small = [
        pltpu.make_async_copy(lengths_in, lengths, small_sem.at[0]),
        pltpu.make_async_copy(outscale_in, outscale, small_sem.at[1]),
        pltpu.make_async_copy(noise_in, noise, small_sem.at[2]),
    ]
    my_rows = pl.ds(pl.multiple_of(core * half, half), half)
    other_rows = pl.ds(pl.multiple_of(other * half, half), half)
    my_cols = pl.ds(pl.multiple_of(core * share, share), share)
    other_cols = pl.ds(pl.multiple_of(other * share, share), share)
    inputs = (points, vectors)
    locals_ = [
        pltpu.make_async_copy(array, columns.at[0, kind, my_rows, :], local_sem.at[kind])
        for kind, array in enumerate(inputs)
    ]
    locals_.append(pltpu.make_async_copy(vectors, mine, local_sem.at[2]))
    for copy in small + locals_:
        copy.start()

    def greets(index):
        if index == 3:
            return spot == 0
        return plane_peer(index) > me

    def answers(index):
        if index == 3:
            return spot == 3
        return plane_peer(index) < me

    barrier = pltpu.get_barrier_semaphore()

    @pl.when(core == 0)
    def _():
        signal(barrier, me, other)

    for index in range(1, PLANE):
        @pl.when(greets(index))
        def _():
            signal(barrier, plane_peer(index), core)

    def greet_line(step):
        @pl.when(line_peer(step) > me)
        def _():
            for feat in range(2):
                signal(barrier, line_peer(step), feat)

    loop(1, line, greet_line)
    before = core + jnp.where(spot == 3, 3, jnp.minimum(spot, 1)) + 2 * level

    @pl.when(before > 0)
    def _():
        pl.semaphore_wait(barrier, before)

    @pl.when(core == 1)
    def _():
        signal(twin_alive, me, other)

    for index in range(1, PLANE):
        @pl.when(answers(index))
        def _():
            signal(plane_alive.at[index], plane_peer(index), core)

    def answer_line(step):
        @pl.when(line_peer(step) < me)
        def _():
            for feat in range(2):
                signal(line_alive.at[step, core], line_peer(step), feat)

    loop(1, line, answer_line)

    pair = [
        remote(array, columns.at[0, kind, my_rows, :], pair_send.at[kind], pair_recv.at[kind],
               me, other)
        for kind, array in enumerate(inputs)
    ]

    def plane_copy(index, kind):
        return remote(inputs[kind], columns.at[index, kind, my_rows, :],
                      plane_send.at[index, kind], plane_recv.at[index, kind],
                      plane_peer(index), core)

    def twin(index, kind):
        place = columns.at[index, kind, my_rows, :]
        return remote(place, place, twin_send.at[index, kind], twin_recv.at[index, kind],
                      me, other)

    def row_copy(step, feat):
        return remote(columns.at[0, 0, my_rows, feat * share:(feat + 1) * share],
                      row_points.at[step, my_rows, :],
                      row_send.at[step, feat], row_recv.at[step, core],
                      line_peer(step), feat)

    def row_arrival(step, feat):
        spots = pl.ds(feat * half, half)
        return remote(columns.at[0, 0, my_rows, 0:share], row_points.at[step, spots, :],
                      row_send.at[step, feat], row_recv.at[step, feat],
                      line_peer(step), feat)

    def send_plane(index):
        for kind in range(2):
            plane_copy(index, kind).start()

    for index in range(1, PLANE):
        @pl.when(answers(index))
        def _():
            send_plane(index)

    def send_low(step):
        @pl.when(line_peer(step) < me)
        def _():
            for feat in range(2):
                row_copy(step, feat).start()

    for copy in locals_:
        copy.wait()
    loop(1, line, send_low)

    @pl.when(core == 0)
    def _():
        pl.semaphore_wait(twin_alive, 1)

    for copy in pair:
        copy.start()

    for index in range(1, PLANE):
        @pl.when(greets(index))
        def _():
            pl.semaphore_wait(plane_alive.at[index], 1)
            send_plane(index)

    @pl.when((spot == 1) | (spot == 2))
    def _():
        send_plane(3)

    def send_high(step):
        @pl.when(line_peer(step) > me)
        def _():
            for feat in range(2):
                pl.semaphore_wait(line_alive.at[step, feat], 1)
                row_copy(step, feat).start()

    for copy in small:
        copy.wait()
    scale = outscale[0]
    top = jnp.log(jnp.full((1, 1), scale, F32)) * LOG2E
    column = jnp.transpose(jnp.broadcast_to(lengths[...], (feats, feats)))[:, 0:1]

    for copy in pair:
        copy.wait_recv()

    def prepare_columns(index):
        for part in range(2):
            cols = slice(part * share, (part + 1) * share)
            guest = (columns[index, 0, :, cols].astype(F32) / column).astype(BF16)
            wide = guest.astype(F32)
            norm = -0.5 * LOG2E * jnp.sum(wide * wide, axis=0, keepdims=True)
            one = jnp.ones_like(norm)
            stacked = jnp.concatenate(
                [guest, guest, guest, extra_rows(pieces(norm) + (one, one, one))], axis=0)
            right[index, cols, :] = stacked.T

    def prepare_rows(step, value):
        scaled = (value.astype(F32) / column).astype(BF16).astype(F32)
        height = -0.5 * LOG2E * jnp.sum(scaled * scaled, axis=0, keepdims=True) + top
        one = jnp.ones_like(height)
        for index, piece in enumerate(pieces(scaled * LOG2E)):
            left[step, index * feats:(index + 1) * feats, :] = piece.astype(BF16)
        left[step, 3 * feats:, :] = extra_rows((one, one, one) + pieces(height))

    def unit(step, index):
        power = jnp.dot(right[index], left[step], preferred_element_type=F32)
        value = jnp.exp2(jnp.minimum(power, top)).astype(BF16)
        return jnp.dot(columns[index, 1], value, preferred_element_type=F32)

    def give_back(step, feat):
        return remote(part_out.at[step, feat], inbox.at[step, core],
                      part_send.at[step, feat], part_recv.at[step, core],
                      line_peer(step), feat)

    def back_arrival(step, feat):
        return remote(part_out.at[step, feat], inbox.at[step, feat],
                      part_send.at[step, feat], part_recv.at[step, feat],
                      line_peer(step), feat)

    def forward(index):
        for kind in range(2):
            plane_copy(index, kind).wait_recv()
            twin(index, kind).start()

    prepare_columns(0)

    def open_row(step):
        for feat in range(2):
            row_arrival(step, feat).wait_recv()
        prepare_rows(step, row_points[step])

    def first(step):
        @pl.when(step == 0)
        def _():
            prepare_rows(step, columns[0, 0, :, my_cols])

        @pl.when(step == 1)
        def _():
            loop(1, line, send_high)
            open_row(step)

        total[step] = unit(step, 0)

    loop(0, 2, first)
    forward(1)

    def upward(place):
        return level ^ (place + jnp.where(place >= level, 1, 0))

    def open_column(index):
        for kind in range(2):
            twin(index, kind).wait_recv()
        prepare_columns(index)

    def add_unit(step, index):
        total[step] += unit(step, index)

    def send_back(step):
        for feat in range(2):
            part_out[step, feat] = (
                total[step, feat * half:(feat + 1) * half, :].astype(BF16))
        for feat in range(2):
            give_back(step, feat).start()

    def rest(place):
        step = jnp.where(place < line - 1, upward(place), 0)

        @pl.when(step > 1)
        def _():
            open_row(step)
            total[step] = unit(step, 0)

        @pl.when(place == 0)
        def _():
            forward(2)

        def one_column(index):
            @pl.when(place == 0)
            def _():
                open_column(index)

            add_unit(step, index)

            @pl.when((place == 0) & (index == 1))
            def _():
                forward(PLANE - 1)

        loop(1, PLANE, one_column)

        @pl.when(place < line - 1)
        def _():
            send_back(step)

    loop(0, line, rest)

    swap_out[...] = total[0, other_rows, :]
    swap = remote(swap_out, swap_in, swap_send, swap_recv, me, other)
    swap.start()
    factor = noise[0]
    result[:, my_cols] = total[0, my_rows, :] + factor * mine[:, my_cols].astype(F32)
    result[:, other_cols] = factor * mine[:, other_cols].astype(F32)

    for copy in pair:
        copy.wait_send()
    for index in range(1, PLANE):
        for kind in range(2):
            plane_copy(index, kind).wait_send()
            twin(index, kind).wait_send()

    def drain(step):
        for feat in range(2):
            give_back(step, feat).wait_send()
            row_copy(step, feat).wait_send()

    loop(1, line, drain)

    def collect(step):
        for feat in range(2):
            back_arrival(step, feat).wait_recv()
            result[:, feat * share:(feat + 1) * share] += inbox[step, feat].astype(F32)

    loop(1, line, collect)
    swap.wait_recv()
    result[:, other_cols] += swap_in[...]

    swap.wait_send()


def per_device(blk, points, vectors, lengthscale, outscale, noise):
    assert blk % (4 * PLANE) == 0 and blk & (blk - 1) == 0
    line = blk // PLANE
    rows, half = points.shape
    feats = 2 * half
    share = rows // 2
    stay = pl.BlockSpec(memory_space=pltpu.HBM)
    vmem = pl.BlockSpec(memory_space=pltpu.VMEM)
    dma = pltpu.SemaphoreType.DMA
    regular = pltpu.SemaphoreType.REGULAR
    wide = 3 * feats + EXTRA
    out = pl.pallas_call(
        functools.partial(kernel, line),
        out_shape=pltpu.VMEM((half, rows), F32),
        in_specs=[stay] * 5,
        out_specs=vmem,
        scratch_shapes=[
            pltpu.VMEM((1, feats), F32),
            pltpu.SMEM((1,), F32),
            pltpu.SMEM((1,), F32),
            dma((3,)),
            pltpu.VMEM((PLANE, 2, feats, rows), BF16),
            pltpu.VMEM((line, feats, share), BF16),
            pltpu.VMEM((PLANE, rows, wide), BF16),
            pltpu.VMEM((line, wide, share), BF16),
            pltpu.VMEM((line, feats, share), F32),
            pltpu.VMEM((line, 2, half, share), BF16),
            pltpu.VMEM((line, 2, half, share), BF16),
            pltpu.VMEM((half, rows), BF16),
            pltpu.VMEM((half, share), F32),
            pltpu.VMEM((half, share), F32),
            regular,
            regular((PLANE,)),
            regular((line, 2)),
            dma((3,)),
            dma((2,)),
            dma((2,)),
            dma((PLANE, 2)),
            dma((PLANE, 2)),
            dma((PLANE, 2)),
            dma((PLANE, 2)),
            dma((line, 2)),
            dma((line, 2)),
            dma((line, 2)),
            dma((line, 2)),
            dma,
            dma,
        ],
        compiler_params=pltpu.CompilerParams(collective_id=0, has_side_effects=True),
        name="tile_solve",
    )(points.T, vectors.T, lengthscale.reshape(1, feats), outscale, noise)
    return out.T


def solution(mesh):
    placed = (P("blk", "feat"), P("blk", "feat"), P(), P(), P())
    return jax.shard_map(
        functools.partial(per_device, mesh.shape["blk"]),
        mesh=mesh, in_specs=placed, out_specs=P("blk", "feat"), check_vma=False,
    )
```

```python
import functools

import jax
import jax.numpy as jnp
from jax import lax
from jax.experimental import pallas as pl
from jax.experimental.pallas import tpu as pltpu
from jax.sharding import PartitionSpec as P

LOG2E = 1.4426950408889634
F32 = jnp.float32
BF16 = jnp.bfloat16
EXTRA = 16
PLANE = 4


def pieces(value):
    first = value.astype(BF16).astype(F32)
    rest = value - first
    second = rest.astype(BF16).astype(F32)
    return first, second, rest - second


def extra_rows(rows):
    shape = (EXTRA, rows[0].shape[1])
    place = lax.broadcasted_iota(jnp.int32, shape, 0)
    out = jnp.zeros(shape, F32)
    for index, row in enumerate(rows):
        out = jnp.where(place == index, row, out)
    return out.astype(BF16)


def kernel(
    line, points, vectors, lengths_in, outscale, noise, result,
    lengths, columns, row_points, right, left, total, part_out, inbox, swap_out, swap_in,
    twin_alive, plane_alive, line_alive,
    small_sem, local_sem, plane_send, pair_recv, plane_recv, twin_send, twin_recv,
    row_send, row_recv, part_send, part_recv, swap_send, swap_recv,
):
    me = lax.axis_index("blk")
    core = lax.axis_index("feat")
    other = 1 - core
    half, rows = points.shape
    feats = 2 * half
    share = rows // 2
    spot = me % PLANE
    level = me // PLANE

    def remote(src, dst, send, arrive, blk, feat):
        return pltpu.make_async_remote_copy(
            src_ref=src, dst_ref=dst, send_sem=send, recv_sem=arrive,
            device_id={"blk": blk, "feat": feat}, device_id_type=pl.DeviceIdType.MESH,
        )

    def signal(sem, blk, feat):
        pl.semaphore_signal(
            sem, inc=1, device_id={"blk": blk, "feat": feat},
            device_id_type=pl.DeviceIdType.MESH,
        )

    def plane_peer(index):
        return me ^ index

    def line_peer(step):
        return me ^ (step * PLANE)

    def loop(first, last, body):
        def one(index, carry):
            body(index)
            return carry
        lax.fori_loop(first, last, one, 0)

    my_rows = pl.ds(pl.multiple_of(core * half, half), half)
    other_rows = pl.ds(pl.multiple_of(other * half, half), half)
    my_cols = pl.ds(pl.multiple_of(core * share, share), share)
    other_cols = pl.ds(pl.multiple_of(other * share, share), share)
    inputs = (points, vectors)
    small = pltpu.make_async_copy(lengths_in, lengths, small_sem)
    small.start()
    for kind, array in enumerate(inputs):
        pltpu.make_async_copy(array, columns.at[0, kind, my_rows, :], local_sem).start()

    def greets(index):
        if index == 3:
            return spot == 0
        return plane_peer(index) > me

    def answers(index):
        if index == 3:
            return spot == 3
        return plane_peer(index) < me

    barrier = pltpu.get_barrier_semaphore()

    @pl.when(core == 0)
    def _():
        signal(barrier, me, other)

    for index in range(1, PLANE):
        @pl.when(greets(index))
        def _():
            signal(barrier, plane_peer(index), core)

    def greet_line(step):
        @pl.when(line_peer(step) > me)
        def _():
            for feat in range(2):
                signal(barrier, line_peer(step), feat)

    loop(1, line, greet_line)
    before = core + jnp.where(spot == 3, 3, jnp.minimum(spot, 1)) + 2 * level

    @pl.when(before > 0)
    def _():
        pl.semaphore_wait(barrier, before)

    @pl.when(core == 1)
    def _():
        signal(twin_alive, me, other)

    for index in range(1, PLANE):
        @pl.when(answers(index))
        def _():
            signal(plane_alive.at[index - 1], plane_peer(index), core)

    def answer_line(step):
        @pl.when(line_peer(step) < me)
        def _():
            for feat in range(2):
                signal(line_alive.at[step - 1], line_peer(step), feat)

    loop(1, line, answer_line)

    def half_of(index):
        return columns.at[index, :, my_rows, :]

    def send_plane(index):
        for kind, array in enumerate(inputs):
            remote(array, columns.at[index, kind, my_rows, :], plane_send,
                   plane_recv.at[index - 1], plane_peer(index), core).start()

    def plane_arrival(index):
        return remote(half_of(index), half_of(index), plane_send, plane_recv.at[index - 1],
                      plane_peer(index), core)

    def twin(index):
        return remote(half_of(index), half_of(index), twin_send, twin_recv.at[index - 1],
                      me, other)

    def send_row(step):
        for feat in range(2):
            remote(columns.at[0, 0, my_rows, feat * share:(feat + 1) * share],
                   row_points.at[step, my_rows, :], row_send, row_recv.at[step - 1],
                   line_peer(step), feat).start()

    def row_arrival(step):
        return remote(row_points.at[step], row_points.at[step], row_send,
                      row_recv.at[step - 1], line_peer(step), core)

    for index in range(1, PLANE):
        @pl.when(answers(index))
        def _():
            send_plane(index)

    def send_low(step):
        @pl.when(line_peer(step) < me)
        def _():
            send_row(step)

    pltpu.make_async_copy(half_of(0), half_of(0), local_sem).wait()
    loop(1, line, send_low)

    @pl.when(core == 0)
    def _():
        pl.semaphore_wait(twin_alive, 1)

    pair = remote(half_of(0), half_of(0), plane_send, pair_recv, me, other)
    pair.start()

    for index in range(1, PLANE):
        @pl.when(greets(index))
        def _():
            pl.semaphore_wait(plane_alive.at[index - 1], 1)
            send_plane(index)

    @pl.when((spot == 1) | (spot == 2))
    def _():
        send_plane(3)

    def send_high(step):
        @pl.when(line_peer(step) > me)
        def _():
            pl.semaphore_wait(line_alive.at[step - 1], 2)
            send_row(step)

    small.wait()
    top = jnp.log(jnp.full((1, 1), outscale[0], F32)) * LOG2E
    column = jnp.transpose(jnp.broadcast_to(lengths[...], (feats, feats)))[:, 0:1]

    pair.wait_recv()

    def prepare_columns(index):
        for part in range(2):
            cols = slice(part * share, (part + 1) * share)
            guest = (columns[index, 0, :, cols].astype(F32) / column).astype(BF16)
            wide = guest.astype(F32)
            norm = -0.5 * LOG2E * jnp.sum(wide * wide, axis=0, keepdims=True)
            one = jnp.ones_like(norm)
            stacked = jnp.concatenate(
                [guest, guest, guest, extra_rows(pieces(norm) + (one, one, one))], axis=0)
            right[index, cols, :] = stacked.T

    def prepare_rows(step, value):
        scaled = (value.astype(F32) / column).astype(BF16).astype(F32)
        height = -0.5 * LOG2E * jnp.sum(scaled * scaled, axis=0, keepdims=True) + top
        one = jnp.ones_like(height)
        for index, piece in enumerate(pieces(scaled * LOG2E)):
            left[step, index * feats:(index + 1) * feats, :] = piece.astype(BF16)
        left[step, 3 * feats:, :] = extra_rows((one, one, one) + pieces(height))

    def unit(step, index):
        power = jnp.dot(right[index], left[step], preferred_element_type=F32)
        value = jnp.exp2(jnp.minimum(power, top)).astype(BF16)
        return jnp.dot(columns[index, 1], value, preferred_element_type=F32)

    def give_back(step, feat):
        return remote(part_out.at[step, feat], inbox.at[step, core], part_send, part_recv,
                      line_peer(step), feat)

    def forward(index):
        plane_arrival(index).wait_recv()
        twin(index).start()

    def open_column(index):
        twin(index).wait_recv()
        prepare_columns(index)

    def open_row(step):
        row_arrival(step).wait_recv()
        prepare_rows(step, row_points[step])

    def add_unit(step, index):
        total[step] += unit(step, index)

    def send_back(step):
        for feat in range(2):
            part_out[step, feat] = (
                total[step, feat * half:(feat + 1) * half, :].astype(BF16))
        for feat in range(2):
            give_back(step, feat).start()

    second = jnp.maximum(level, 2)
    prepare_columns(0)

    def first(place):
        step = jnp.where(place == 2, second, place)

        @pl.when(place == 0)
        def _():
            prepare_rows(step, columns[0, 0, :, my_cols])

        @pl.when(place == 1)
        def _():
            loop(1, line, send_high)

        @pl.when(place > 0)
        def _():
            open_row(step)

        total[step] = unit(step, 0)

        for index in range(1, PLANE - 1):
            @pl.when(place == index)
            def _():
                forward(index)

    loop(0, 3, first)

    own = jnp.where(level == 0, 1, 0)

    def rest(place):
        step = level ^ (place + jnp.where(place >= level, 1, 0))
        step = jnp.where(level < 2, place + 1, step)
        step = jnp.where(place < line - 1, step, 0)

        @pl.when((step > 1) & (step != second))
        def _():
            open_row(step)
            total[step] = unit(step, 0)

        def one_column(index):
            @pl.when(place == 0)
            def _():
                open_column(index)

            add_unit(step, index)

            @pl.when((place == 0) & (index == 1))
            def _():
                loop(0, own, lambda _: add_unit(0, 1))
                forward(PLANE - 1)

        loop(jnp.where(place < line - 1, 1, 1 + own), PLANE, one_column)

        @pl.when(place < line - 1)
        def _():
            send_back(step)

    loop(0, line, rest)

    swap_out[...] = total[0, other_rows, :]
    swap = remote(swap_out, swap_in, swap_send, swap_recv, me, other)
    swap.start()
    factor = noise[0]
    mine = columns.at[0, 1, my_rows, :]
    result[:, my_cols] = total[0, my_rows, :] + factor * mine[:, my_cols].astype(F32)
    result[:, other_cols] = factor * mine[:, other_cols].astype(F32)

    whole = columns.at[:, :, my_rows, :]
    remote(whole, whole, plane_send, pair_recv, me, other).wait_send()
    guests = columns.at[1:PLANE, :, my_rows, :]
    remote(guests, guests, twin_send, pair_recv, me, other).wait_send()
    given = row_points.at[1:line]
    remote(given, given, row_send, pair_recv, me, other).wait_send()
    back = remote(part_out.at[1:line], inbox.at[1:line], part_send, part_recv, me, other)
    back.wait_send()
    back.wait_recv()

    def collect(step):
        for feat in range(2):
            result[:, feat * share:(feat + 1) * share] += inbox[step, feat].astype(F32)

    loop(1, line, collect)
    swap.wait_recv()
    result[:, other_cols] += swap_in[...]
    swap.wait_send()


def per_device(blk, points, vectors, lengthscale, outscale, noise):
    assert blk % (4 * PLANE) == 0 and blk & (blk - 1) == 0
    line = blk // PLANE
    rows, half = points.shape
    feats = 2 * half
    share = rows // 2
    stay = pl.BlockSpec(memory_space=pltpu.HBM)
    scalar = pl.BlockSpec(memory_space=pltpu.SMEM)
    vmem = pl.BlockSpec(memory_space=pltpu.VMEM)
    dma = pltpu.SemaphoreType.DMA
    regular = pltpu.SemaphoreType.REGULAR
    wide = 3 * feats + EXTRA
    out = pl.pallas_call(
        functools.partial(kernel, line),
        out_shape=pltpu.VMEM((half, rows), F32),
        in_specs=[stay] * 3 + [scalar] * 2,
        out_specs=vmem,
        scratch_shapes=[
            pltpu.VMEM((1, feats), F32),
            pltpu.VMEM((PLANE, 2, feats, rows), BF16),
            pltpu.VMEM((line, feats, share), BF16),
            pltpu.VMEM((PLANE, rows, wide), BF16),
            pltpu.VMEM((line, wide, share), BF16),
            pltpu.VMEM((line, feats, share), F32),
            pltpu.VMEM((line, 2, half, share), BF16),
            pltpu.VMEM((line, 2, half, share), BF16),
            pltpu.VMEM((half, share), F32),
            pltpu.VMEM((half, share), F32),
            regular,
            regular((PLANE - 1,)),
            regular((line - 1,)),
            dma,
            dma,
            dma,
            dma,
            dma((PLANE - 1,)),
            dma,
            dma((PLANE - 1,)),
            dma,
            dma((line - 1,)),
            dma,
            dma,
            dma,
            dma,
        ],
        compiler_params=pltpu.CompilerParams(collective_id=0, has_side_effects=True),
        name="tile_solve",
    )(points.T, vectors.T, lengthscale.reshape(1, feats), outscale, noise)
    return out.T


def solution(mesh):
    placed = (P("blk", "feat"), P("blk", "feat"), P(), P(), P())
    return jax.shard_map(
        functools.partial(per_device, mesh.shape["blk"]),
        mesh=mesh, in_specs=placed, out_specs=P("blk", "feat"), check_vma=False,
    )
```

```python
import functools

import jax
import jax.numpy as jnp
from jax import lax
from jax.experimental import pallas as pl
from jax.experimental.pallas import tpu as pltpu
from jax.sharding import PartitionSpec as P

LOG2E = 1.4426950408889634
F32 = jnp.float32
BF16 = jnp.bfloat16
EXTRA = 16
PLANE = 4


def pieces(value):
    first = value.astype(BF16).astype(F32)
    rest = value - first
    second = rest.astype(BF16).astype(F32)
    return first, second, rest - second


def extra_rows(rows):
    shape = (EXTRA, rows[0].shape[1])
    place = lax.broadcasted_iota(jnp.int32, shape, 0)
    out = jnp.zeros(shape, F32)
    for index, row in enumerate(rows):
        out = jnp.where(place == index, row, out)
    return out.astype(BF16)


def kernel(
    line, points, vectors, lengths_in, outscale, noise, result,
    lengths, columns, row_points, right, left, total, part_out, inbox, swap_out, swap_in,
    twin_alive, plane_alive, line_alive,
    small_sem, local_sem, plane_send, pair_recv, plane_recv, twin_send, twin_recv,
    row_send, row_recv, part_send, part_recv, swap_send, swap_recv,
):
    me = lax.axis_index("blk")
    core = lax.axis_index("feat")
    other = 1 - core
    half, rows = points.shape
    feats = 2 * half
    share = rows // 2
    spot = me % PLANE
    level = me // PLANE

    def remote(src, dst, send, arrive, blk, feat):
        return pltpu.make_async_remote_copy(
            src_ref=src, dst_ref=dst, send_sem=send, recv_sem=arrive,
            device_id={"blk": blk, "feat": feat}, device_id_type=pl.DeviceIdType.MESH,
        )

    def signal(sem, blk, feat):
        pl.semaphore_signal(
            sem, inc=1, device_id={"blk": blk, "feat": feat},
            device_id_type=pl.DeviceIdType.MESH,
        )

    def plane_peer(index):
        return me ^ index

    def line_peer(step):
        return me ^ (step * PLANE)

    def loop(first, last, body):
        def one(index, carry):
            body(index)
            return carry
        lax.fori_loop(first, last, one, 0)

    my_rows = pl.ds(pl.multiple_of(core * half, half), half)
    other_rows = pl.ds(pl.multiple_of(other * half, half), half)
    my_cols = pl.ds(pl.multiple_of(core * share, share), share)
    other_cols = pl.ds(pl.multiple_of(other * share, share), share)
    inputs = (points, vectors)
    small = pltpu.make_async_copy(lengths_in, lengths, small_sem)
    small.start()
    for kind, array in enumerate(inputs):
        pltpu.make_async_copy(array, columns.at[0, kind, my_rows, :], local_sem).start()

    def greets(index):
        if index == 3:
            return spot == 0
        return plane_peer(index) > me

    def answers(index):
        if index == 3:
            return spot == 3
        return plane_peer(index) < me

    barrier = pltpu.get_barrier_semaphore()

    @pl.when(core == 0)
    def _():
        signal(barrier, me, other)

    for index in range(1, PLANE):
        @pl.when(greets(index))
        def _():
            signal(barrier, plane_peer(index), core)

    def greet_line(step):
        @pl.when(line_peer(step) > me)
        def _():
            for feat in range(2):
                signal(barrier, line_peer(step), feat)

    loop(1, line, greet_line)
    before = core + jnp.where(spot == 3, 3, jnp.minimum(spot, 1)) + 2 * level

    @pl.when(before > 0)
    def _():
        pl.semaphore_wait(barrier, before)

    @pl.when(core == 1)
    def _():
        signal(twin_alive, me, other)

    for index in range(1, PLANE):
        @pl.when(answers(index))
        def _():
            signal(plane_alive.at[index - 1], plane_peer(index), core)

    def answer_line(step):
        @pl.when(line_peer(step) < me)
        def _():
            for feat in range(2):
                signal(line_alive.at[step - 1], line_peer(step), feat)

    loop(1, line, answer_line)

    def half_of(index):
        return columns.at[index, :, my_rows, :]

    def send_plane(index):
        for kind, array in enumerate(inputs):
            remote(array, columns.at[index, kind, my_rows, :], plane_send,
                   plane_recv.at[index - 1], plane_peer(index), core).start()

    def plane_arrival(index):
        return remote(half_of(index), half_of(index), plane_send, plane_recv.at[index - 1],
                      plane_peer(index), core)

    def twin(index):
        return remote(half_of(index), half_of(index), twin_send, twin_recv.at[index - 1],
                      me, other)

    def send_row(step):
        for feat in range(2):
            remote(columns.at[0, 0, my_rows, feat * share:(feat + 1) * share],
                   row_points.at[step, my_rows, :], row_send, row_recv.at[step - 1],
                   line_peer(step), feat).start()

    def row_arrival(step):
        return remote(row_points.at[step], row_points.at[step], row_send,
                      row_recv.at[step - 1], line_peer(step), core)

    for index in range(1, PLANE):
        @pl.when(answers(index))
        def _():
            send_plane(index)

    def send_low(step):
        @pl.when(line_peer(step) < me)
        def _():
            send_row(step)

    pltpu.make_async_copy(half_of(0), half_of(0), local_sem).wait()
    loop(1, line, send_low)

    @pl.when(core == 0)
    def _():
        pl.semaphore_wait(twin_alive, 1)

    pair = remote(half_of(0), half_of(0), plane_send, pair_recv, me, other)
    pair.start()

    for index in range(1, PLANE):
        @pl.when(greets(index))
        def _():
            pl.semaphore_wait(plane_alive.at[index - 1], 1)
            send_plane(index)

    @pl.when((spot == 1) | (spot == 2))
    def _():
        send_plane(3)

    def send_high(step):
        @pl.when(line_peer(step) > me)
        def _():
            pl.semaphore_wait(line_alive.at[step - 1], 2)
            send_row(step)

    loop(1, line, send_high)
    small.wait()
    top = jnp.log(jnp.full((1, 1), outscale[0], F32)) * LOG2E
    column = jnp.transpose(jnp.broadcast_to(lengths[...], (feats, feats)))[:, 0:1]

    pair.wait_recv()

    def prepare_columns(index):
        for part in range(2):
            cols = slice(part * share, (part + 1) * share)
            guest = (columns[index, 0, :, cols].astype(F32) / column).astype(BF16)
            wide = guest.astype(F32)
            norm = -0.5 * LOG2E * jnp.sum(wide * wide, axis=0, keepdims=True)
            one = jnp.ones_like(norm)
            stacked = jnp.concatenate(
                [guest, guest, guest, extra_rows(pieces(norm) + (one, one, one))], axis=0)
            right[index, cols, :] = stacked.T

    def prepare_rows(step, value):
        scaled = (value.astype(F32) / column).astype(BF16).astype(F32)
        height = -0.5 * LOG2E * jnp.sum(scaled * scaled, axis=0, keepdims=True) + top
        one = jnp.ones_like(height)
        for index, piece in enumerate(pieces(scaled * LOG2E)):
            left[step, index * feats:(index + 1) * feats, :] = piece.astype(BF16)
        left[step, 3 * feats:, :] = extra_rows((one, one, one) + pieces(height))

    def unit(step, index):
        power = jnp.dot(right[index], left[step], preferred_element_type=F32)
        value = jnp.exp2(jnp.minimum(power, top)).astype(BF16)
        return jnp.dot(columns[index, 1], value, preferred_element_type=F32)

    def span(step, start):
        guests = right[start:].reshape((PLANE - start) * rows, right.shape[2])
        power = jnp.dot(guests, left[step], preferred_element_type=F32)
        value = jnp.exp2(jnp.minimum(power, top)).astype(BF16)
        return sum(
            jnp.dot(columns[start + place, 1], value[place * rows:(place + 1) * rows],
                    preferred_element_type=F32)
            for place in range(PLANE - start))

    def give_back(step, feat):
        return remote(part_out.at[step, feat], inbox.at[step, core], part_send, part_recv,
                      line_peer(step), feat)

    def forward(index):
        plane_arrival(index).wait_recv()
        twin(index).start()

    def open_column(index):
        twin(index).wait_recv()
        prepare_columns(index)

    def open_row(step):
        row_arrival(step).wait_recv()
        prepare_rows(step, row_points[step])

    def add_unit(step, index):
        total[step] += unit(step, index)

    def send_back(step):
        for feat in range(2):
            part_out[step, feat] = (
                total[step, feat * half:(feat + 1) * half, :].astype(BF16))
        for feat in range(2):
            give_back(step, feat).start()

    second = jnp.maximum(level, 2)
    prepare_columns(0)

    def first(place):
        step = jnp.where(place == 2, second, place)

        @pl.when(place == 0)
        def _():
            prepare_rows(step, columns[0, 0, :, my_cols])

        @pl.when(place > 0)
        def _():
            open_row(step)

        total[step] = unit(step, 0)

        for index in range(1, PLANE - 1):
            @pl.when(place == index)
            def _():
                forward(index)

    loop(0, 3, first)

    own = jnp.where(level == 0, 1, 0)

    def rest(place):
        step = level ^ (place + jnp.where(place >= level, 1, 0))
        step = jnp.where(level == 1, place + 1, step)
        step = jnp.where(level == 0, jnp.where(place < line - 2, place + 2, 1), step)
        step = jnp.where(place < line - 1, step, 0)

        fresh = (step > 1) & (step != second)
        alone = (place == 0) | ((place == line - 1) & (level == 0))

        @pl.when(fresh)
        def _():
            open_row(step)
            total[step] = span(step, 0)

        @pl.when(jnp.logical_not(fresh | alone))
        def _():
            total[step] += span(step, 1)

        def one_column(index):
            @pl.when(place == 0)
            def _():
                open_column(index)

            add_unit(step, index)

            @pl.when((place == 0) & (index == 1))
            def _():
                loop(0, own, lambda _: add_unit(0, 1))
                forward(PLANE - 1)

        loop(jnp.where(alone, jnp.where(place == 0, 1, 2), PLANE), PLANE, one_column)

        @pl.when(place < line - 1)
        def _():
            send_back(step)

    loop(0, line, rest)

    swap_out[...] = total[0, other_rows, :]
    swap = remote(swap_out, swap_in, swap_send, swap_recv, me, other)
    swap.start()
    factor = noise[0]
    mine = columns.at[0, 1, my_rows, :]
    result[:, my_cols] = total[0, my_rows, :] + factor * mine[:, my_cols].astype(F32)
    result[:, other_cols] = factor * mine[:, other_cols].astype(F32)

    whole = columns.at[:, :, my_rows, :]
    remote(whole, whole, plane_send, pair_recv, me, other).wait_send()
    guests = columns.at[1:PLANE, :, my_rows, :]
    remote(guests, guests, twin_send, pair_recv, me, other).wait_send()
    given = row_points.at[1:line]
    remote(given, given, row_send, pair_recv, me, other).wait_send()
    back = remote(part_out.at[1:line], inbox.at[1:line], part_send, part_recv, me, other)
    back.wait_send()
    back.wait_recv()

    def collect(step):
        for feat in range(2):
            result[:, feat * share:(feat + 1) * share] += inbox[step, feat].astype(F32)

    loop(1, line, collect)
    swap.wait_recv()
    result[:, other_cols] += swap_in[...]
    swap.wait_send()


def per_device(blk, points, vectors, lengthscale, outscale, noise):
    assert blk % (4 * PLANE) == 0 and blk & (blk - 1) == 0
    line = blk // PLANE
    rows, half = points.shape
    feats = 2 * half
    share = rows // 2
    stay = pl.BlockSpec(memory_space=pltpu.HBM)
    scalar = pl.BlockSpec(memory_space=pltpu.SMEM)
    vmem = pl.BlockSpec(memory_space=pltpu.VMEM)
    dma = pltpu.SemaphoreType.DMA
    regular = pltpu.SemaphoreType.REGULAR
    wide = 3 * feats + EXTRA
    out = pl.pallas_call(
        functools.partial(kernel, line),
        out_shape=pltpu.VMEM((half, rows), F32),
        in_specs=[stay] * 3 + [scalar] * 2,
        out_specs=vmem,
        scratch_shapes=[
            pltpu.VMEM((1, feats), F32),
            pltpu.VMEM((PLANE, 2, feats, rows), BF16),
            pltpu.VMEM((line, feats, share), BF16),
            pltpu.VMEM((PLANE, rows, wide), BF16),
            pltpu.VMEM((line, wide, share), BF16),
            pltpu.VMEM((line, feats, share), F32),
            pltpu.VMEM((line, 2, half, share), BF16),
            pltpu.VMEM((line, 2, half, share), BF16),
            pltpu.VMEM((half, share), F32),
            pltpu.VMEM((half, share), F32),
            regular,
            regular((PLANE - 1,)),
            regular((line - 1,)),
            dma,
            dma,
            dma,
            dma,
            dma((PLANE - 1,)),
            dma,
            dma((PLANE - 1,)),
            dma,
            dma((line - 1,)),
            dma,
            dma,
            dma,
            dma,
        ],
        compiler_params=pltpu.CompilerParams(collective_id=0, has_side_effects=True),
        name="tile_solve",
    )(points.T, vectors.T, lengthscale.reshape(1, feats), outscale, noise)
    return out.T


def solution(mesh):
    placed = (P("blk", "feat"), P("blk", "feat"), P(), P(), P())
    return jax.shard_map(
        functools.partial(per_device, mesh.shape["blk"]),
        mesh=mesh, in_specs=placed, out_specs=P("blk", "feat"), check_vma=False,
    )
```

```python
import functools

import jax
import jax.numpy as jnp
from jax import lax
from jax.experimental import pallas as pl
from jax.experimental.pallas import tpu as pltpu
from jax.sharding import PartitionSpec as P

LOG2E = 1.4426950408889634
F32 = jnp.float32
BF16 = jnp.bfloat16
EXTRA = 16
PLANE = 4


def pieces(value):
    first = value.astype(BF16).astype(F32)
    rest = value - first
    second = rest.astype(BF16).astype(F32)
    return first, second, rest - second


def extra_rows(rows):
    shape = (EXTRA, rows[0].shape[1])
    place = lax.broadcasted_iota(jnp.int32, shape, 0)
    out = jnp.zeros(shape, F32)
    for index, row in enumerate(rows):
        out = jnp.where(place == index, row, out)
    return out.astype(BF16)


def kernel(
    line, points, vectors, lengths_in, outscale, noise, result,
    lengths, columns, row_points, right, left, total, held, part_out, inbox, swap_out, swap_in,
    twin_alive, plane_alive, line_alive,
    small_sem, local_sem, plane_send, pair_recv, plane_recv, twin_send, twin_recv,
    row_send, row_recv, part_send, part_recv, swap_send, swap_recv,
):
    me = lax.axis_index("blk")
    core = lax.axis_index("feat")
    other = 1 - core
    half, rows = points.shape
    feats = 2 * half
    share = rows // 2
    spot = me % PLANE
    level = me // PLANE

    def remote(src, dst, send, arrive, blk, feat):
        return pltpu.make_async_remote_copy(
            src_ref=src, dst_ref=dst, send_sem=send, recv_sem=arrive,
            device_id={"blk": blk, "feat": feat}, device_id_type=pl.DeviceIdType.MESH,
        )

    def signal(sem, blk, feat):
        pl.semaphore_signal(
            sem, inc=1, device_id={"blk": blk, "feat": feat},
            device_id_type=pl.DeviceIdType.MESH,
        )

    def plane_peer(index):
        return me ^ index

    def line_peer(step):
        return me ^ (step * PLANE)

    def loop(first, last, body):
        def one(index, carry):
            body(index)
            return carry
        lax.fori_loop(first, last, one, 0)

    my_rows = pl.ds(pl.multiple_of(core * half, half), half)
    other_rows = pl.ds(pl.multiple_of(other * half, half), half)
    my_cols = pl.ds(pl.multiple_of(core * share, share), share)
    other_cols = pl.ds(pl.multiple_of(other * share, share), share)
    inputs = (points, vectors)
    small = pltpu.make_async_copy(lengths_in, lengths, small_sem)
    small.start()
    for kind, array in enumerate(inputs):
        pltpu.make_async_copy(array, columns.at[0, kind, my_rows, :], local_sem).start()

    def greets(index):
        if index == 3:
            return spot == 0
        return plane_peer(index) > me

    def answers(index):
        if index == 3:
            return spot == 3
        return plane_peer(index) < me

    barrier = pltpu.get_barrier_semaphore()

    @pl.when(core == 0)
    def _():
        signal(barrier, me, other)

    for index in range(1, PLANE):
        @pl.when(greets(index))
        def _():
            signal(barrier, plane_peer(index), core)

    def greet_line(step):
        @pl.when(line_peer(step) > me)
        def _():
            for feat in range(2):
                signal(barrier, line_peer(step), feat)

    loop(1, line, greet_line)
    before = core + jnp.where(spot == 3, 3, jnp.minimum(spot, 1)) + 2 * level

    @pl.when(before > 0)
    def _():
        pl.semaphore_wait(barrier, before)

    @pl.when(core == 1)
    def _():
        signal(twin_alive, me, other)

    for index in range(1, PLANE):
        @pl.when(answers(index))
        def _():
            signal(plane_alive.at[index - 1], plane_peer(index), core)

    def answer_line(step):
        @pl.when(line_peer(step) < me)
        def _():
            for feat in range(2):
                signal(line_alive.at[step - 1], line_peer(step), feat)

    loop(1, line, answer_line)

    def half_of(index):
        return columns.at[index, :, my_rows, :]

    def slot(index, kind):
        return PLANE - 1 if kind == 1 and index == PLANE - 1 else index - 1

    def part_of(index, kind):
        return half_of(index) if kind is None else columns.at[index, kind, my_rows, :]

    def send_plane(index):
        target = index
        if index > 1:
            target = jnp.where(spot ^ index == 2, 5 - index, index)
        for kind, array in enumerate(inputs):
            arrive = target - 1
            if index > 1 and kind == 1:
                arrive = jnp.where(target == PLANE - 1, PLANE - 1, target - 1)
            remote(array, columns.at[target, kind, my_rows, :], plane_send,
                   plane_recv.at[arrive], plane_peer(index), core).start()

    def plane_arrival(index, kind=None):
        place = part_of(index, kind)
        return remote(place, place, plane_send, plane_recv.at[slot(index, kind)],
                      plane_peer(index), core)

    def twin(index, kind=None):
        place = part_of(index, kind)
        return remote(place, place, twin_send, twin_recv.at[slot(index, kind)], me, other)

    def send_row(step):
        for feat in range(2):
            remote(columns.at[0, 0, my_rows, feat * share:(feat + 1) * share],
                   row_points.at[step, my_rows, :], row_send, row_recv.at[step - 1],
                   line_peer(step), feat).start()

    def row_arrival(step):
        return remote(row_points.at[step], row_points.at[step], row_send,
                      row_recv.at[step - 1], line_peer(step), core)

    for index in range(1, PLANE):
        @pl.when(answers(index))
        def _():
            send_plane(index)

    def send_low(step):
        @pl.when(line_peer(step) < me)
        def _():
            send_row(step)

    pltpu.make_async_copy(half_of(0), half_of(0), local_sem).wait()
    loop(1, line, send_low)

    @pl.when(core == 0)
    def _():
        pl.semaphore_wait(twin_alive, 1)

    pair = remote(half_of(0), half_of(0), plane_send, pair_recv, me, other)
    pair.start()

    for index in range(1, PLANE):
        @pl.when(greets(index))
        def _():
            pl.semaphore_wait(plane_alive.at[index - 1], 1)
            send_plane(index)

    @pl.when((spot == 1) | (spot == 2))
    def _():
        send_plane(3)

    def send_high(step):
        @pl.when(line_peer(step) > me)
        def _():
            pl.semaphore_wait(line_alive.at[step - 1], 2)
            send_row(step)

    loop(1, line, send_high)
    small.wait()
    top = jnp.log(jnp.full((1, 1), outscale[0], F32)) * LOG2E
    column = jnp.transpose(jnp.broadcast_to(lengths[...], (feats, feats)))[:, 0:1]

    pair.wait_recv()

    def prepare_columns(index):
        for part in range(2):
            cols = slice(part * share, (part + 1) * share)
            guest = (columns[index, 0, :, cols].astype(F32) / column).astype(BF16)
            wide = guest.astype(F32)
            norm = -0.5 * LOG2E * jnp.sum(wide * wide, axis=0, keepdims=True)
            one = jnp.ones_like(norm)
            stacked = jnp.concatenate(
                [guest, guest, guest, extra_rows(pieces(norm) + (one, one, one))], axis=0)
            right[index, cols, :] = stacked.T

    def prepare_rows(step, value):
        scaled = (value.astype(F32) / column).astype(BF16).astype(F32)
        height = -0.5 * LOG2E * jnp.sum(scaled * scaled, axis=0, keepdims=True) + top
        one = jnp.ones_like(height)
        for index, piece in enumerate(pieces(scaled * LOG2E)):
            left[step, index * feats:(index + 1) * feats, :] = piece.astype(BF16)
        left[step, 3 * feats:, :] = extra_rows((one, one, one) + pieces(height))

    def entries(step, index):
        power = jnp.dot(right[index], left[step], preferred_element_type=F32)
        return jnp.exp2(jnp.minimum(power, top)).astype(BF16)

    def unit(step, index):
        return jnp.dot(columns[index, 1], entries(step, index), preferred_element_type=F32)

    def span(step, start):
        guests = right[start:].reshape((PLANE - start) * rows, right.shape[2])
        power = jnp.dot(guests, left[step], preferred_element_type=F32)
        value = jnp.exp2(jnp.minimum(power, top)).astype(BF16)
        return sum(
            jnp.dot(columns[start + place, 1], value[place * rows:(place + 1) * rows],
                    preferred_element_type=F32)
            for place in range(PLANE - start))

    def give_back(step, feat):
        return remote(part_out.at[step, feat], inbox.at[step, core], part_send, part_recv,
                      line_peer(step), feat)

    def forward(index, kind=None):
        plane_arrival(index, kind).wait_recv()
        twin(index, kind).start()

    def open_column(index, kind=None):
        twin(index, kind).wait_recv()
        prepare_columns(index)

    def open_row(step):
        row_arrival(step).wait_recv()
        prepare_rows(step, row_points[step])

    def add_unit(step, index):
        total[step] += unit(step, index)

    def send_back(step):
        for feat in range(2):
            part_out[step, feat] = (
                total[step, feat * half:(feat + 1) * half, :].astype(BF16))
        for feat in range(2):
            give_back(step, feat).start()

    second = jnp.maximum(level, 2)
    prepare_columns(0)

    def first(place):
        step = jnp.where(place == 2, second, place)

        @pl.when(place == 0)
        def _():
            prepare_rows(step, columns[0, 0, :, my_cols])

        @pl.when(place > 0)
        def _():
            open_row(step)

        total[step] = unit(step, 0)

        for index in range(1, PLANE - 1):
            @pl.when(place == index)
            def _():
                forward(index)

    loop(0, 3, first)

    own = jnp.where(level == 0, 1, 0)
    soon = (core == 1) | (spot == 2)

    def rest(place):
        step = level ^ (place + jnp.where(place >= level, 1, 0))
        step = jnp.where(level == 1, place + 1, step)
        step = jnp.where(level == 0, jnp.where(place < line - 2, place + 2, 1), step)
        step = jnp.where(place < line - 1, step, 0)

        fresh = (step > 1) & (step != second)
        alone = (place == 0) | ((place == line - 1) & (level == 0))

        @pl.when(fresh)
        def _():
            open_row(step)
            total[step] = span(step, 0)

        @pl.when(jnp.logical_not(fresh | alone))
        def _():
            total[step] += span(step, 1)

        def one_column(index):
            @pl.when((place == 0) & (index < PLANE - 1))
            def _():
                open_column(index)

            add_unit(step, index)

            @pl.when((place == 0) & (index == 1))
            def _():
                loop(0, own, lambda _: add_unit(0, 1))
                forward(PLANE - 1, 0)

            @pl.when((place == 0) & (index == jnp.where(soon, 1, PLANE - 2)))
            def _():
                forward(PLANE - 1, 1)

        loop(jnp.where(alone, jnp.where(place == 0, 1, 2), PLANE),
             jnp.where(place == 0, PLANE - 1, PLANE), one_column)

        @pl.when(place == 0)
        def _():
            open_column(PLANE - 1, 0)
            held[...] = entries(step, PLANE - 1)
            twin(PLANE - 1, 1).wait_recv()
            total[step] += jnp.dot(columns[PLANE - 1, 1], held[...],
                                   preferred_element_type=F32)

        @pl.when(place < line - 1)
        def _():
            send_back(step)

    loop(0, line, rest)

    swap_out[...] = total[0, other_rows, :]
    swap = remote(swap_out, swap_in, swap_send, swap_recv, me, other)
    swap.start()
    factor = noise[0]
    mine = columns.at[0, 1, my_rows, :]
    result[:, my_cols] = total[0, my_rows, :] + factor * mine[:, my_cols].astype(F32)
    result[:, other_cols] = factor * mine[:, other_cols].astype(F32)

    whole = columns.at[:, :, my_rows, :]
    remote(whole, whole, plane_send, pair_recv, me, other).wait_send()
    guests = columns.at[1:PLANE, :, my_rows, :]
    remote(guests, guests, twin_send, pair_recv, me, other).wait_send()
    given = row_points.at[1:line]
    remote(given, given, row_send, pair_recv, me, other).wait_send()
    back = remote(part_out.at[1:line], inbox.at[1:line], part_send, part_recv, me, other)
    back.wait_send()
    back.wait_recv()

    def collect(step):
        for feat in range(2):
            result[:, feat * share:(feat + 1) * share] += inbox[step, feat].astype(F32)

    loop(1, line, collect)
    swap.wait_recv()
    result[:, other_cols] += swap_in[...]
    swap.wait_send()


def per_device(blk, points, vectors, lengthscale, outscale, noise):
    assert blk % (4 * PLANE) == 0 and blk & (blk - 1) == 0
    line = blk // PLANE
    rows, half = points.shape
    feats = 2 * half
    share = rows // 2
    stay = pl.BlockSpec(memory_space=pltpu.HBM)
    scalar = pl.BlockSpec(memory_space=pltpu.SMEM)
    vmem = pl.BlockSpec(memory_space=pltpu.VMEM)
    dma = pltpu.SemaphoreType.DMA
    regular = pltpu.SemaphoreType.REGULAR
    wide = 3 * feats + EXTRA
    out = pl.pallas_call(
        functools.partial(kernel, line),
        out_shape=pltpu.VMEM((half, rows), F32),
        in_specs=[stay] * 3 + [scalar] * 2,
        out_specs=vmem,
        scratch_shapes=[
            pltpu.VMEM((1, feats), F32),
            pltpu.VMEM((PLANE, 2, feats, rows), BF16),
            pltpu.VMEM((line, feats, share), BF16),
            pltpu.VMEM((PLANE, rows, wide), BF16),
            pltpu.VMEM((line, wide, share), BF16),
            pltpu.VMEM((line, feats, share), F32),
            pltpu.VMEM((rows, share), BF16),
            pltpu.VMEM((line, 2, half, share), BF16),
            pltpu.VMEM((line, 2, half, share), BF16),
            pltpu.VMEM((half, share), F32),
            pltpu.VMEM((half, share), F32),
            regular,
            regular((PLANE - 1,)),
            regular((line - 1,)),
            dma,
            dma,
            dma,
            dma,
            dma((PLANE,)),
            dma,
            dma((PLANE,)),
            dma,
            dma((line - 1,)),
            dma,
            dma,
            dma,
            dma,
        ],
        compiler_params=pltpu.CompilerParams(collective_id=0, has_side_effects=True),
        name="tile_solve",
    )(points.T, vectors.T, lengthscale.reshape(1, feats), outscale, noise)
    return out.T


def solution(mesh):
    placed = (P("blk", "feat"), P("blk", "feat"), P(), P(), P())
    return jax.shard_map(
        functools.partial(per_device, mesh.shape["blk"]),
        mesh=mesh, in_specs=placed, out_specs=P("blk", "feat"), check_vma=False,
    )
```

```python
import functools

import jax
import jax.numpy as jnp
from jax import lax
from jax.experimental import pallas as pl
from jax.experimental.pallas import tpu as pltpu
from jax.sharding import PartitionSpec as P

LOG2E = 1.4426950408889634
F32 = jnp.float32
BF16 = jnp.bfloat16
EXTRA = 16
PLANE = 4


def pieces(value):
    first = value.astype(BF16).astype(F32)
    rest = value - first
    second = rest.astype(BF16).astype(F32)
    return first, second, rest - second


def extra_rows(rows):
    shape = (EXTRA, rows[0].shape[1])
    place = lax.broadcasted_iota(jnp.int32, shape, 0)
    out = jnp.zeros(shape, F32)
    for index, row in enumerate(rows):
        out = jnp.where(place == index, row, out)
    return out.astype(BF16)


def kernel(
    line, points, vectors, lengths_in, outscale, noise, result,
    lengths, columns, row_points, right, left, total, held, part_out, inbox, swap_out, swap_in,
    twin_alive, plane_alive, line_alive,
    small_sem, local_sem, plane_send, pair_recv, plane_recv, twin_send, twin_recv,
    row_send, row_recv, part_send, part_recv, swap_send, swap_recv,
):
    me = lax.axis_index("blk")
    core = lax.axis_index("feat")
    other = 1 - core
    half, rows = points.shape
    feats = 2 * half
    share = rows // 2
    spot = me % PLANE
    level = me // PLANE

    def remote(src, dst, send, arrive, blk, feat):
        return pltpu.make_async_remote_copy(
            src_ref=src, dst_ref=dst, send_sem=send, recv_sem=arrive,
            device_id={"blk": blk, "feat": feat}, device_id_type=pl.DeviceIdType.MESH,
        )

    def signal(sem, blk, feat):
        pl.semaphore_signal(
            sem, inc=1, device_id={"blk": blk, "feat": feat},
            device_id_type=pl.DeviceIdType.MESH,
        )

    def plane_peer(index):
        return me ^ index

    def line_peer(step):
        return me ^ (step * PLANE)

    def loop(first, last, body):
        def one(index, carry):
            body(index)
            return carry
        lax.fori_loop(first, last, one, 0)

    my_rows = pl.ds(pl.multiple_of(core * half, half), half)
    other_rows = pl.ds(pl.multiple_of(other * half, half), half)
    my_cols = pl.ds(pl.multiple_of(core * share, share), share)
    other_cols = pl.ds(pl.multiple_of(other * share, share), share)
    inputs = (points, vectors)
    small = pltpu.make_async_copy(lengths_in, lengths, small_sem)
    small.start()
    for kind, array in enumerate(inputs):
        pltpu.make_async_copy(array, columns.at[0, kind, my_rows, :], local_sem).start()

    def greets(index):
        if index == 3:
            return spot == 0
        return plane_peer(index) > me

    def answers(index):
        if index == 3:
            return spot == 3
        return plane_peer(index) < me

    barrier = pltpu.get_barrier_semaphore()

    @pl.when(core == 0)
    def _():
        signal(barrier, me, other)

    for index in range(1, PLANE):
        @pl.when(greets(index))
        def _():
            signal(barrier, plane_peer(index), core)

    def greet_line(step):
        @pl.when(line_peer(step) > me)
        def _():
            for feat in range(2):
                signal(barrier, line_peer(step), feat)

    loop(1, line, greet_line)
    before = core + jnp.where(spot == 3, 3, jnp.minimum(spot, 1)) + 2 * level

    @pl.when(before > 0)
    def _():
        pl.semaphore_wait(barrier, before)

    @pl.when(core == 1)
    def _():
        signal(twin_alive, me, other)

    for index in range(1, PLANE):
        @pl.when(answers(index))
        def _():
            signal(plane_alive.at[index - 1], plane_peer(index), core)

    def answer_line(step):
        @pl.when(line_peer(step) < me)
        def _():
            for feat in range(2):
                signal(line_alive.at[step - 1], line_peer(step), feat)

    loop(1, line, answer_line)

    def half_of(index):
        return columns.at[index, :, my_rows, :]

    def slot(index, kind):
        return PLANE - 1 if kind == 1 and index == PLANE - 1 else index - 1

    def part_of(index, kind):
        if kind is None:
            return half_of(index)
        return columns.at[index, kind, :, my_cols]

    def send_plane(index):
        for kind, array in enumerate(inputs):
            remote(array, columns.at[index, kind, my_rows, :], plane_send,
                   plane_recv.at[index - 1], plane_peer(index), core).start()

    def send_last():
        for kind in range(2):
            remote(part_of(0, kind), part_of(PLANE - 1, kind), plane_send,
                   plane_recv.at[slot(PLANE - 1, kind)], plane_peer(PLANE - 1), core).start()

    def plane_arrival(index, kind=None):
        place = part_of(index, kind)
        return remote(place, place, plane_send, plane_recv.at[slot(index, kind)],
                      plane_peer(index), core)

    def twin(index, kind=None):
        place = part_of(index, kind)
        return remote(place, place, twin_send, twin_recv.at[slot(index, kind)], me, other)

    def send_row(step):
        for feat in range(2):
            remote(columns.at[0, 0, my_rows, feat * share:(feat + 1) * share],
                   row_points.at[step, my_rows, :], row_send, row_recv.at[step - 1],
                   line_peer(step), feat).start()

    def row_arrival(step):
        return remote(row_points.at[step], row_points.at[step], row_send,
                      row_recv.at[step - 1], line_peer(step), core)

    for index in range(1, PLANE - 1):
        @pl.when(answers(index))
        def _():
            send_plane(index)

    def send_low(step):
        @pl.when(line_peer(step) < me)
        def _():
            send_row(step)

    pltpu.make_async_copy(half_of(0), half_of(0), local_sem).wait()
    loop(1, line, send_low)

    @pl.when(core == 0)
    def _():
        pl.semaphore_wait(twin_alive, 1)

    pair = remote(half_of(0), half_of(0), plane_send, pair_recv, me, other)
    pair.start()

    for index in range(1, PLANE - 1):
        @pl.when(greets(index))
        def _():
            pl.semaphore_wait(plane_alive.at[index - 1], 1)
            send_plane(index)

    @pl.when(greets(PLANE - 1))
    def _():
        pl.semaphore_wait(plane_alive.at[PLANE - 2], 1)

    pair.wait_recv()
    send_last()

    def send_high(step):
        @pl.when(line_peer(step) > me)
        def _():
            pl.semaphore_wait(line_alive.at[step - 1], 2)
            send_row(step)

    loop(1, line, send_high)
    small.wait()
    top = jnp.log(jnp.full((1, 1), outscale[0], F32)) * LOG2E
    column = jnp.transpose(jnp.broadcast_to(lengths[...], (feats, feats)))[:, 0:1]

    def prepare_columns(index, parts=(slice(0, share), slice(share, rows))):
        for cols in parts:
            guest = (columns[index, 0, :, cols].astype(F32) / column).astype(BF16)
            wide = guest.astype(F32)
            norm = -0.5 * LOG2E * jnp.sum(wide * wide, axis=0, keepdims=True)
            one = jnp.ones_like(norm)
            stacked = jnp.concatenate(
                [guest, guest, guest, extra_rows(pieces(norm) + (one, one, one))], axis=0)
            right[index, cols, :] = stacked.T

    def prepare_rows(step, value):
        scaled = (value.astype(F32) / column).astype(BF16).astype(F32)
        height = -0.5 * LOG2E * jnp.sum(scaled * scaled, axis=0, keepdims=True) + top
        one = jnp.ones_like(height)
        for index, piece in enumerate(pieces(scaled * LOG2E)):
            left[step, index * feats:(index + 1) * feats, :] = piece.astype(BF16)
        left[step, 3 * feats:, :] = extra_rows((one, one, one) + pieces(height))

    def entries(step, guests):
        power = jnp.dot(guests, left[step], preferred_element_type=F32)
        return jnp.exp2(jnp.minimum(power, top)).astype(BF16)

    def unit(step, index):
        return jnp.dot(columns[index, 1], entries(step, right[index]),
                       preferred_element_type=F32)

    def span(step, start):
        guests = right[start:].reshape((PLANE - start) * rows, right.shape[2])
        value = entries(step, guests)
        return sum(
            jnp.dot(columns[start + place, 1], value[place * rows:(place + 1) * rows],
                    preferred_element_type=F32)
            for place in range(PLANE - start))

    def give_back(step, feat):
        return remote(part_out.at[step, feat], inbox.at[step, core], part_send, part_recv,
                      line_peer(step), feat)

    def forward(index, kind=None):
        plane_arrival(index, kind).wait_recv()
        twin(index, kind).start()

    def open_column(index):
        twin(index).wait_recv()
        prepare_columns(index)

    def open_row(step):
        row_arrival(step).wait_recv()
        prepare_rows(step, row_points[step])

    def add_unit(step, index):
        total[step] += unit(step, index)

    def send_back(step):
        for feat in range(2):
            part_out[step, feat] = (
                total[step, feat * half:(feat + 1) * half, :].astype(BF16))
        for feat in range(2):
            give_back(step, feat).start()

    second = jnp.maximum(level, 2)
    prepare_columns(0)

    def first(place):
        step = jnp.where(place == 2, second, place)

        @pl.when(place == 0)
        def _():
            prepare_rows(step, columns[0, 0, :, my_cols])

        @pl.when(place > 0)
        def _():
            open_row(step)

        total[step] = unit(step, 0)

        for index in range(1, PLANE - 1):
            @pl.when(place == index)
            def _():
                forward(index)

    loop(0, 3, first)

    own = jnp.where(level == 0, 1, 0)
    soon = (core == 1) | (spot == 2)

    last = PLANE - 1

    def own_half(step):
        prepare_columns(last, (my_cols,))
        total[step] += jnp.dot(
            columns[last, 1, :, my_cols], entries(step, right[last, my_cols, :]),
            preferred_element_type=F32)

    def rest(place):
        step = level ^ (place + jnp.where(place >= level, 1, 0))
        step = jnp.where(level == 1, place + 1, step)
        step = jnp.where(level == 0, jnp.where(place < line - 2, place + 2, 1), step)
        step = jnp.where(place < line - 1, step, 0)

        fresh = (step > 1) & (step != second)
        alone = (place == 0) | ((place == line - 1) & (level == 0))

        @pl.when(fresh)
        def _():
            open_row(step)
            total[step] = span(step, 0)

        @pl.when(jnp.logical_not(fresh | alone))
        def _():
            total[step] += span(step, 1)

        def one_column(index):
            @pl.when((place == 0) & (index < PLANE - 1))
            def _():
                open_column(index)

            add_unit(step, index)

            @pl.when((place == 0) & (index == 1))
            def _():
                loop(0, own, lambda _: add_unit(0, 1))
                forward(PLANE - 1, 0)

            @pl.when((place == 0) & (index == jnp.where(soon, 1, PLANE - 2)))
            def _():
                forward(PLANE - 1, 1)

            @pl.when(soon & (place == 0) & (index == 1))
            def _():
                own_half(step)

        loop(jnp.where(alone, jnp.where(place == 0, 1, 2), PLANE),
             jnp.where(place == 0, PLANE - 1, PLANE), one_column)

        @pl.when(place == 0)
        def _():
            @pl.when(jnp.logical_not(soon))
            def _():
                own_half(step)

            twin(last, 0).wait_recv()
            prepare_columns(last, (other_cols,))
            held[...] = entries(step, right[last, other_cols, :])
            twin(last, 1).wait_recv()
            total[step] += jnp.dot(columns[last, 1, :, other_cols], held[...],
                                   preferred_element_type=F32)

        @pl.when(place < line - 1)
        def _():
            send_back(step)

    loop(0, line, rest)

    swap_out[...] = total[0, other_rows, :]
    swap = remote(swap_out, swap_in, swap_send, swap_recv, me, other)
    swap.start()
    factor = noise[0]
    mine = columns.at[0, 1, my_rows, :]
    result[:, my_cols] = total[0, my_rows, :] + factor * mine[:, my_cols].astype(F32)
    result[:, other_cols] = factor * mine[:, other_cols].astype(F32)

    whole = columns.at[:, :, my_rows, :]
    remote(whole, whole, plane_send, pair_recv, me, other).wait_send()
    guests = columns.at[1:PLANE, :, my_rows, :]
    remote(guests, guests, twin_send, pair_recv, me, other).wait_send()
    given = row_points.at[1:line]
    remote(given, given, row_send, pair_recv, me, other).wait_send()
    back = remote(part_out.at[1:line], inbox.at[1:line], part_send, part_recv, me, other)
    back.wait_send()
    back.wait_recv()

    def collect(step):
        for feat in range(2):
            result[:, feat * share:(feat + 1) * share] += inbox[step, feat].astype(F32)

    loop(1, line, collect)
    swap.wait_recv()
    result[:, other_cols] += swap_in[...]
    swap.wait_send()


def per_device(blk, points, vectors, lengthscale, outscale, noise):
    assert blk % (4 * PLANE) == 0 and blk & (blk - 1) == 0
    line = blk // PLANE
    rows, half = points.shape
    feats = 2 * half
    share = rows // 2
    stay = pl.BlockSpec(memory_space=pltpu.HBM)
    scalar = pl.BlockSpec(memory_space=pltpu.SMEM)
    vmem = pl.BlockSpec(memory_space=pltpu.VMEM)
    dma = pltpu.SemaphoreType.DMA
    regular = pltpu.SemaphoreType.REGULAR
    wide = 3 * feats + EXTRA
    out = pl.pallas_call(
        functools.partial(kernel, line),
        out_shape=pltpu.VMEM((half, rows), F32),
        in_specs=[stay] * 3 + [scalar] * 2,
        out_specs=vmem,
        scratch_shapes=[
            pltpu.VMEM((1, feats), F32),
            pltpu.VMEM((PLANE, 2, feats, rows), BF16),
            pltpu.VMEM((line, feats, share), BF16),
            pltpu.VMEM((PLANE, rows, wide), BF16),
            pltpu.VMEM((line, wide, share), BF16),
            pltpu.VMEM((line, feats, share), F32),
            pltpu.VMEM((share, share), BF16),
            pltpu.VMEM((line, 2, half, share), BF16),
            pltpu.VMEM((line, 2, half, share), BF16),
            pltpu.VMEM((half, share), F32),
            pltpu.VMEM((half, share), F32),
            regular,
            regular((PLANE - 1,)),
            regular((line - 1,)),
            dma,
            dma,
            dma,
            dma,
            dma((PLANE,)),
            dma,
            dma((PLANE,)),
            dma,
            dma((line - 1,)),
            dma,
            dma,
            dma,
            dma,
        ],
        compiler_params=pltpu.CompilerParams(collective_id=0, has_side_effects=True),
        name="tile_solve",
    )(points.T, vectors.T, lengthscale.reshape(1, feats), outscale, noise)
    return out.T


def solution(mesh):
    placed = (P("blk", "feat"), P("blk", "feat"), P(), P(), P())
    return jax.shard_map(
        functools.partial(per_device, mesh.shape["blk"]),
        mesh=mesh, in_specs=placed, out_specs=P("blk", "feat"), check_vma=False,
    )
```

```python
import functools

import jax
import jax.numpy as jnp
from jax import lax
from jax.experimental import pallas as pl
from jax.experimental.pallas import tpu as pltpu
from jax.sharding import PartitionSpec as P

LOG2E = 1.4426950408889634
F32 = jnp.float32
BF16 = jnp.bfloat16
EXTRA = 16
PLANE = 4


def pieces(value):
    first = value.astype(BF16).astype(F32)
    rest = value - first
    second = rest.astype(BF16).astype(F32)
    return first, second, rest - second


def extra_rows(rows):
    shape = (EXTRA, rows[0].shape[1])
    place = lax.broadcasted_iota(jnp.int32, shape, 0)
    out = jnp.zeros(shape, F32)
    for index, row in enumerate(rows):
        out = jnp.where(place == index, row, out)
    return out.astype(BF16)


def kernel(
    line, points, vectors, lengths_in, outscale, noise, result,
    lengths, columns, row_points, right, left, total, held, part_out, inbox, swap_out, swap_in,
    twin_alive, plane_alive, line_alive,
    small_sem, local_sem, plane_send, pair_recv, plane_recv, twin_send, twin_recv,
    row_send, row_recv, part_send, part_recv, swap_send, swap_recv,
):
    me = lax.axis_index("blk")
    core = lax.axis_index("feat")
    other = 1 - core
    half, rows = points.shape
    feats = 2 * half
    share = rows // 2
    spot = me % PLANE
    level = me // PLANE

    def remote(src, dst, send, arrive, blk, feat):
        return pltpu.make_async_remote_copy(
            src_ref=src, dst_ref=dst, send_sem=send, recv_sem=arrive,
            device_id={"blk": blk, "feat": feat}, device_id_type=pl.DeviceIdType.MESH,
        )

    def signal(sem, blk, feat):
        pl.semaphore_signal(
            sem, inc=1, device_id={"blk": blk, "feat": feat},
            device_id_type=pl.DeviceIdType.MESH,
        )

    def plane_peer(index):
        return me ^ index

    def line_peer(step):
        return me ^ (step * PLANE)

    def loop(first, last, body):
        def one(index, carry):
            body(index)
            return carry
        lax.fori_loop(first, last, one, 0)

    my_rows = pl.ds(pl.multiple_of(core * half, half), half)
    other_rows = pl.ds(pl.multiple_of(other * half, half), half)
    my_cols = pl.ds(pl.multiple_of(core * share, share), share)
    other_cols = pl.ds(pl.multiple_of(other * share, share), share)
    inputs = (points, vectors)
    small = pltpu.make_async_copy(lengths_in, lengths, small_sem)
    small.start()
    for kind, array in enumerate(inputs):
        pltpu.make_async_copy(array, columns.at[0, kind, my_rows, :], local_sem).start()

    def greets(index):
        if index == 3:
            return spot == 0
        return plane_peer(index) > me

    def answers(index):
        if index == 3:
            return spot == 3
        return plane_peer(index) < me

    barrier = pltpu.get_barrier_semaphore()

    @pl.when(core == 0)
    def _():
        signal(barrier, me, other)

    for index in range(1, PLANE):
        @pl.when(greets(index))
        def _():
            signal(barrier, plane_peer(index), core)

    def greet_line(step):
        @pl.when(line_peer(step) > me)
        def _():
            for feat in range(2):
                signal(barrier, line_peer(step), feat)

    loop(1, line, greet_line)
    before = core + jnp.where(spot == 3, 3, jnp.minimum(spot, 1)) + 2 * level

    @pl.when(before > 0)
    def _():
        pl.semaphore_wait(barrier, before)

    @pl.when(core == 1)
    def _():
        signal(twin_alive, me, other)

    for index in range(1, PLANE):
        @pl.when(answers(index))
        def _():
            signal(plane_alive.at[index - 1], plane_peer(index), core)

    def answer_line(step):
        @pl.when(line_peer(step) < me)
        def _():
            for feat in range(2):
                signal(line_alive.at[step - 1], line_peer(step), feat)

    loop(1, line, answer_line)

    def half_of(index):
        return columns.at[index, :, my_rows, :]

    def slot(index, kind):
        return PLANE - 1 if kind == 1 and index == PLANE - 1 else index - 1

    def part_of(index, kind):
        return half_of(index) if kind is None else columns.at[index, kind, my_rows, :]

    def send_plane(index, kept=True):
        target = index
        if index > 1:
            target = jnp.where(spot ^ index == 2, 5 - index, index)
        for kind, array in enumerate(inputs):
            arrive = target - 1
            if index > 1 and kind == 1:
                arrive = jnp.where(target == PLANE - 1, PLANE - 1, target - 1)
            source = columns.at[0, kind, my_rows, :] if kept else array
            remote(source, columns.at[target, kind, my_rows, :], plane_send,
                   plane_recv.at[arrive], plane_peer(index), core).start()

    def plane_arrival(index, kind=None):
        place = part_of(index, kind)
        return remote(place, place, plane_send, plane_recv.at[slot(index, kind)],
                      plane_peer(index), core)

    def twin(index, kind=None):
        place = part_of(index, kind)
        return remote(place, place, twin_send, twin_recv.at[slot(index, kind)], me, other)

    def send_row(step):
        for feat in range(2):
            remote(columns.at[0, 0, my_rows, feat * share:(feat + 1) * share],
                   row_points.at[step, my_rows, :], row_send, row_recv.at[step - 1],
                   line_peer(step), feat).start()

    def row_arrival(step):
        return remote(row_points.at[step], row_points.at[step], row_send,
                      row_recv.at[step - 1], line_peer(step), core)

    pltpu.make_async_copy(half_of(0), half_of(0), local_sem).wait()
    for index in range(1, PLANE):
        @pl.when(answers(index))
        def _():
            send_plane(index)

    def send_low(step):
        @pl.when(line_peer(step) < me)
        def _():
            send_row(step)

    loop(1, line, send_low)

    @pl.when(core == 0)
    def _():
        pl.semaphore_wait(twin_alive, 1)

    pair = remote(half_of(0), half_of(0), plane_send, pair_recv, me, other)
    pair.start()

    for index in range(1, PLANE):
        @pl.when(greets(index))
        def _():
            pl.semaphore_wait(plane_alive.at[index - 1], 1)
            send_plane(index)

    @pl.when((spot == 1) | (spot == 2))
    def _():
        send_plane(3)

    def send_high(step):
        @pl.when(line_peer(step) > me)
        def _():
            pl.semaphore_wait(line_alive.at[step - 1], 2)
            send_row(step)

    loop(1, line, send_high)
    small.wait()
    top = jnp.log(jnp.full((1, 1), outscale[0], F32)) * LOG2E
    column = jnp.transpose(jnp.broadcast_to(lengths[...], (feats, feats)))[:, 0:1]

    pair.wait_recv()

    def prepare_columns(index):
        for part in range(2):
            cols = slice(part * share, (part + 1) * share)
            guest = (columns[index, 0, :, cols].astype(F32) / column).astype(BF16)
            wide = guest.astype(F32)
            norm = -0.5 * LOG2E * jnp.sum(wide * wide, axis=0, keepdims=True)
            one = jnp.ones_like(norm)
            stacked = jnp.concatenate(
                [guest, guest, guest, extra_rows(pieces(norm) + (one, one, one))], axis=0)
            right[index, cols, :] = stacked.T

    def prepare_rows(step, value):
        scaled = (value.astype(F32) / column).astype(BF16).astype(F32)
        height = -0.5 * LOG2E * jnp.sum(scaled * scaled, axis=0, keepdims=True) + top
        one = jnp.ones_like(height)
        for index, piece in enumerate(pieces(scaled * LOG2E)):
            left[step, index * feats:(index + 1) * feats, :] = piece.astype(BF16)
        left[step, 3 * feats:, :] = extra_rows((one, one, one) + pieces(height))

    def entries(step, index):
        power = jnp.dot(right[index], left[step], preferred_element_type=F32)
        return jnp.exp2(jnp.minimum(power, top)).astype(BF16)

    def unit(step, index):
        return jnp.dot(columns[index, 1], entries(step, index), preferred_element_type=F32)

    def span(step, start):
        guests = right[start:].reshape((PLANE - start) * rows, right.shape[2])
        power = jnp.dot(guests, left[step], preferred_element_type=F32)
        value = jnp.exp2(jnp.minimum(power, top)).astype(BF16)
        return sum(
            jnp.dot(columns[start + place, 1], value[place * rows:(place + 1) * rows],
                    preferred_element_type=F32)
            for place in range(PLANE - start))

    def give_back(step, feat):
        return remote(part_out.at[step, feat], inbox.at[step, core], part_send, part_recv,
                      line_peer(step), feat)

    def forward(index, kind=None):
        plane_arrival(index, kind).wait_recv()
        twin(index, kind).start()

    def open_column(index, kind=None):
        twin(index, kind).wait_recv()
        prepare_columns(index)

    def open_row(step):
        row_arrival(step).wait_recv()
        prepare_rows(step, row_points[step])

    def add_unit(step, index):
        total[step] += unit(step, index)

    def send_back(step):
        for feat in range(2):
            part_out[step, feat] = (
                total[step, feat * half:(feat + 1) * half, :].astype(BF16))
        for feat in range(2):
            give_back(step, feat).start()

    second = jnp.maximum(level, 2)
    prepare_columns(0)

    def first(place):
        step = jnp.where(place == 2, second, place)

        @pl.when(place == 0)
        def _():
            prepare_rows(step, columns[0, 0, :, my_cols])

        @pl.when(place > 0)
        def _():
            open_row(step)

        total[step] = unit(step, 0)

        for index in range(1, PLANE - 1):
            @pl.when(place == index)
            def _():
                forward(index)

    loop(0, 3, first)

    own = jnp.where(level == 0, 1, 0)
    soon = (core == 1) | (spot == 2)

    def rest(place):
        step = level ^ (place + jnp.where(place >= level, 1, 0))
        step = jnp.where(level == 1, place + 1, step)
        step = jnp.where(level == 0, jnp.where(place < line - 2, place + 2, 1), step)
        step = jnp.where(place < line - 1, step, 0)

        fresh = (step > 1) & (step != second)
        alone = (place == 0) | ((place == line - 1) & (level == 0))

        @pl.when(fresh)
        def _():
            open_row(step)
            total[step] = span(step, 0)

        @pl.when(jnp.logical_not(fresh | alone))
        def _():
            total[step] += span(step, 1)

        def one_column(index):
            @pl.when((place == 0) & (index < PLANE - 1))
            def _():
                open_column(index)

            add_unit(step, index)

            @pl.when((place == 0) & (index == 1))
            def _():
                loop(0, own, lambda _: add_unit(0, 1))
                forward(PLANE - 1, 0)

            @pl.when((place == 0) & (index == jnp.where(soon, 1, PLANE - 2)))
            def _():
                forward(PLANE - 1, 1)

        loop(jnp.where(alone, jnp.where(place == 0, 1, 2), PLANE),
             jnp.where(place == 0, PLANE - 1, PLANE), one_column)

        @pl.when(place == 0)
        def _():
            open_column(PLANE - 1, 0)
            held[...] = entries(step, PLANE - 1)
            twin(PLANE - 1, 1).wait_recv()
            total[step] += jnp.dot(columns[PLANE - 1, 1], held[...],
                                   preferred_element_type=F32)

        @pl.when(place < line - 1)
        def _():
            send_back(step)

    loop(0, line, rest)

    swap_out[...] = total[0, other_rows, :]
    swap = remote(swap_out, swap_in, swap_send, swap_recv, me, other)
    swap.start()
    factor = noise[0]
    mine = columns.at[0, 1, my_rows, :]
    result[:, my_cols] = total[0, my_rows, :] + factor * mine[:, my_cols].astype(F32)
    result[:, other_cols] = factor * mine[:, other_cols].astype(F32)

    whole = columns.at[:, :, my_rows, :]
    remote(whole, whole, plane_send, pair_recv, me, other).wait_send()
    guests = columns.at[1:PLANE, :, my_rows, :]
    remote(guests, guests, twin_send, pair_recv, me, other).wait_send()
    given = row_points.at[1:line]
    remote(given, given, row_send, pair_recv, me, other).wait_send()
    back = remote(part_out.at[1:line], inbox.at[1:line], part_send, part_recv, me, other)
    back.wait_send()
    back.wait_recv()

    def collect(step):
        for feat in range(2):
            result[:, feat * share:(feat + 1) * share] += inbox[step, feat].astype(F32)

    loop(1, line, collect)
    swap.wait_recv()
    result[:, other_cols] += swap_in[...]
    swap.wait_send()


def per_device(blk, points, vectors, lengthscale, outscale, noise):
    assert blk % (4 * PLANE) == 0 and blk & (blk - 1) == 0
    line = blk // PLANE
    rows, half = points.shape
    feats = 2 * half
    share = rows // 2
    stay = pl.BlockSpec(memory_space=pltpu.HBM)
    scalar = pl.BlockSpec(memory_space=pltpu.SMEM)
    vmem = pl.BlockSpec(memory_space=pltpu.VMEM)
    dma = pltpu.SemaphoreType.DMA
    regular = pltpu.SemaphoreType.REGULAR
    wide = 3 * feats + EXTRA
    out = pl.pallas_call(
        functools.partial(kernel, line),
        out_shape=pltpu.VMEM((half, rows), F32),
        in_specs=[stay] * 3 + [scalar] * 2,
        out_specs=vmem,
        scratch_shapes=[
            pltpu.VMEM((1, feats), F32),
            pltpu.VMEM((PLANE, 2, feats, rows), BF16),
            pltpu.VMEM((line, feats, share), BF16),
            pltpu.VMEM((PLANE, rows, wide), BF16),
            pltpu.VMEM((line, wide, share), BF16),
            pltpu.VMEM((line, feats, share), F32),
            pltpu.VMEM((rows, share), BF16),
            pltpu.VMEM((line, 2, half, share), BF16),
            pltpu.VMEM((line, 2, half, share), BF16),
            pltpu.VMEM((half, share), F32),
            pltpu.VMEM((half, share), F32),
            regular,
            regular((PLANE - 1,)),
            regular((line - 1,)),
            dma,
            dma,
            dma,
            dma,
            dma((PLANE,)),
            dma,
            dma((PLANE,)),
            dma,
            dma((line - 1,)),
            dma,
            dma,
            dma,
            dma,
        ],
        compiler_params=pltpu.CompilerParams(collective_id=0, has_side_effects=True),
        name="tile_solve",
    )(points.T, vectors.T, lengthscale.reshape(1, feats), outscale, noise)
    return out.T


def solution(mesh):
    placed = (P("blk", "feat"), P("blk", "feat"), P(), P(), P())
    return jax.shard_map(
        functools.partial(per_device, mesh.shape["blk"]),
        mesh=mesh, in_specs=placed, out_specs=P("blk", "feat"), check_vma=False,
    )
```
